256 devices in a mesh: req: 32 (over z_lo, y, x), tp: 8 (over z_hi, core).
Axes of the slice: x: 4, y: 4, z: 8 (z_hi: 4, z_lo: 2; z = z_hi * 2 + z_lo), core: 2. Of those that a mesh axis runs over, the one named last changes fastest.
Arguments:
- queries: bfloat16 [8192, 1024], P('req', 'tp'), may hold values from -8 to 8
- suffix_kv: bfloat16 [8192, 512], P('req'), may hold values from -6 to 6
- ssm_x: bfloat16 [8192, 3072], P('req', 'tp'), may hold values from -6 to 6
- ssm_z: bfloat16 [8192, 3072], P('req', 'tp'), may hold values from -6 to 6
- ssm_bc: bfloat16 [8192, 512], P('req'), may hold values from -1.5 to 1.5
- ssm_dt: float32 [8192, 24], P('req', 'tp'), may hold values from 0 to 1, as said below
- a_log: float32 [24], P('tp'), may hold values from -0.5 to 0.5
- d_skip: float32 [24], P('tp'), may hold values from 0.5 to 1.5
- prefix_kv: bfloat16 [32, 4096, 512], P('req'), may hold values from -10 to 10
- prefix_end_states: bfloat16 [32, 24, 128, 256], P('req', 'tp'), may hold values from -1.5 to 1.5
- w_attn_out: bfloat16 [1024, 3072], P('tp'), may hold values from -0.1875 to 0.1875
- w_ssm_out: bfloat16 [3072, 3072], P('tp'), may hold values from -0.109375 to 0.109375
- suffix_len: int32 [32], P('req'), may hold values from 32 to 256, as said below
- prefix_of: int32 [32], P('req'), may hold values from 0 to 3
- prefix_owner: int32 [4], replicated, may hold values from 0 to 31, as said below
Outputs:
- mixed: bfloat16 [8192, 3072], P(('req', 'tp'))
- end_state: float32 [32, 24, 128, 256], P('req', 'tp')
The draws below stay inside these ranges and needn't reach their ends.
Inputs may be any that keep to these rules, and one draw needn't show every extreme that they name: `suffix_len`: some request has the full 256 tokens. `prefix_owner`: distinct slots. `ssm_dt`: positive.
All inputs are finite; a program needn't handle non-finite values.
Results may differ from the reference program's by a relative error of at most 0.014.
Values may be sent and summed in bfloat16 or wider, within the bound.
No kernel may reach another device: no remote copies, remote signals or barrier semaphores. Data moves between devices by JAX's collectives and lax.ppermute only.
A program may use at most 128 MiB of HBM per device.

```python
import jax
import jax.numpy as jnp
from jax import lax

D = 3072
HEAD_SIZE = 128
QH = 8
KEY_VALUE_HEADS = 2
MAMBA_HEADS = 24
MAMBA_STATE_SIZE = 256
PREFIX_LENGTH = 4096
SUFFIX_TOKENS = 256
CH = 256
PREFIX_COUNT = 4
CACHE_SLOTS = 32
REQUEST_COUNT = 32
TOKENS = 8192
N_TP = 8


def draw_queries(key, part):
    value_matrix = jnp.clip(2.0 * jax.random.normal(key, (TOKENS, QH * HEAD_SIZE), jnp.float32), -8.0, 8.0)
    return value_matrix.astype(jnp.bfloat16)


def draw_prefix_kv(key, part):
    array_shape = (CACHE_SLOTS, PREFIX_LENGTH, KEY_VALUE_HEADS * 2 * HEAD_SIZE)
    value_matrix = jnp.clip(jax.random.normal(key, array_shape, jnp.float32), -6.0, 6.0)
    return value_matrix.astype(jnp.bfloat16)


def draw_ssm_dt(key, part):
    key_matrix = jax.random.split(key, 7)
    fast_share = 0.5
    fast = jax.random.uniform(key_matrix[0], (MAMBA_HEADS,)) < fast_share
    fast_base = jnp.exp(jax.random.uniform(key_matrix[1], (MAMBA_HEADS,), jnp.float32, jnp.log(0.75), jnp.log(1.33))) / 40.0
    slow_base = jnp.exp(jax.random.uniform(key_matrix[2], (MAMBA_HEADS,), jnp.float32, jnp.log(0.05), 0.0)) / SUFFIX_TOKENS
    base_offset = jnp.where(fast, fast_base, slow_base)
    request_multiplier = jnp.exp(jax.random.uniform(key_matrix[3], (REQUEST_COUNT, 1, MAMBA_HEADS), jnp.float32, jnp.log(0.5), jnp.log(2.0)))
    approximate = jax.random.uniform(key_matrix[4], (REQUEST_COUNT, SUFFIX_TOKENS, MAMBA_HEADS), jnp.float32, 0.5, 2.0)
    group_positions = jax.random.randint(key_matrix[5], (REQUEST_COUNT, 3), 0, SUFFIX_TOKENS)
    group_token_rows = jnp.repeat(jnp.arange(REQUEST_COUNT), 3)
    group_row_mask = jnp.zeros((REQUEST_COUNT, SUFFIX_TOKENS), jnp.float32).at[group_token_rows, group_positions.reshape(-1)].set(1.0)
    group_row_size = jax.random.uniform(key_matrix[6], (REQUEST_COUNT, SUFFIX_TOKENS, MAMBA_HEADS), jnp.float32, 0.3, 0.45)
    value_matrix = base_offset[None, None, :] * request_multiplier * approximate + group_row_mask[:, :, None] * group_row_size
    return value_matrix.reshape(TOKENS, MAMBA_HEADS)


def draw_suffix_len(key, part):
    lengths = jax.random.randint(key, (REQUEST_COUNT,), SUFFIX_TOKENS // 8, SUFFIX_TOKENS + 1)
    spot = jax.random.randint(jax.random.fold_in(key, 7), (), 0, REQUEST_COUNT)
    return lengths.at[spot].set(SUFFIX_TOKENS).astype(jnp.int32)


def draw_prefix_owner(key, part):
    midpoint = jax.random.permutation(key, CACHE_SLOTS - 2)[:PREFIX_COUNT - 2] + 1
    end_points = jnp.array([0, CACHE_SLOTS - 1], jnp.int32)
    picked = jnp.concatenate([end_points, midpoint.astype(jnp.int32)])
    order = jax.random.permutation(jax.random.fold_in(key, 3), PREFIX_COUNT)
    return picked[order].astype(jnp.int32)


def with_ends(result, rng, smallest, top_value):
    spot = [jax.random.randint(jax.random.fold_in(rng, axis), (), 0, length) for axis, length in enumerate(result.shape)]
    widest = result.shape.index(max(result.shape))
    beside = spot[:widest] + [(spot[widest] + 1) % result.shape[widest]] + spot[widest + 1:]
    return result.at[tuple(spot)].set(smallest).at[tuple(beside)].set(top_value)


def steps_of(own_key, shape, cuts, smallest, high):
    def one(dim, shards_of):
        heights = jax.random.uniform(jax.random.fold_in(jax.random.fold_in(own_key, 6), dim), (shards_of,), jnp.float32, smallest / len(cuts), high / len(cuts))
        return jnp.repeat(jnp.exp(heights), shape[dim] // shards_of).reshape((-1,) + (1,) * (len(shape) - dim - 1))

    level = one(*cuts[0])
    for cut in cuts[1:]:
        level = level * one(*cut)
    return level


def gaussian(rng, dims, spread, limit, cuts=(), kind=jnp.bfloat16):
    drawn = spread * jax.random.normal(rng, dims, jnp.float32)
    if cuts:
        drawn = drawn * steps_of(rng, dims, cuts, -0.22, 0.18)
    return jnp.clip(drawn, -limit, limit).astype(kind)


def setup_inputs(seed: int = 0) -> dict:
    splits = jax.random.split(jax.random.key(seed), 16)
    return {
        "queries": draw_queries(jax.random.fold_in(splits[15], 71), 0),
        "suffix_kv": gaussian(splits[1], (TOKENS, KEY_VALUE_HEADS * 2 * HEAD_SIZE), 1.0, 6.0, ((0, 32),)),
        "ssm_x": gaussian(splits[2], (TOKENS, MAMBA_HEADS * HEAD_SIZE), 1.0, 6.0, ((0, 32), (1, 8))),
        "ssm_z": gaussian(splits[3], (TOKENS, MAMBA_HEADS * HEAD_SIZE), 1.0, 6.0, ((0, 32), (1, 8))),
        "ssm_bc": gaussian(splits[4], (TOKENS, 2 * MAMBA_STATE_SIZE), 0.25, 1.5, ((0, 32),)),
        "ssm_dt": draw_ssm_dt(jax.random.fold_in(splits[15], 71), 0),
        "a_log": jnp.clip(jax.random.uniform(splits[6], (MAMBA_HEADS,), jnp.float32, -0.5, 0.5) * steps_of(splits[6], (MAMBA_HEADS,), ((0, 8),), -0.4, 0.0), -0.5, 0.5),
        "d_skip": jnp.clip(1.0 + 0.1 * jax.random.normal(splits[7], (MAMBA_HEADS,), jnp.float32), 0.5, 1.5),
        "prefix_kv": draw_prefix_kv(jax.random.fold_in(splits[15], 71), 0),
        "prefix_end_states": gaussian(splits[9], (CACHE_SLOTS, MAMBA_HEADS, HEAD_SIZE, MAMBA_STATE_SIZE), 0.25, 1.5, ((0, 32), (1, 8))),
        "w_attn_out": gaussian(splits[10], (QH * HEAD_SIZE, D), (QH * HEAD_SIZE) ** -0.5, 0.1875, ((0, 8),)),
        "w_ssm_out": gaussian(splits[11], (MAMBA_HEADS * HEAD_SIZE, D), (MAMBA_HEADS * HEAD_SIZE) ** -0.5, 0.109375, ((0, 8),)),
        "suffix_len": draw_suffix_len(jax.random.fold_in(splits[15], 71), 0),
        "prefix_of": with_ends(jax.random.randint(splits[13], (REQUEST_COUNT,), 0, PREFIX_COUNT), jax.random.fold_in(splits[13], 1), 0, PREFIX_COUNT - 1).astype(jnp.int32),
        "prefix_owner": draw_prefix_owner(jax.random.fold_in(splits[15], 71), 0),
    }


highest = lax.Precision.HIGHEST


def advance(ssm_state, x_rows, b_rows, c_rows, dt_rows, decay_rate):
    wide_type = dt_rows.dtype
    span = x_rows.shape[0]
    position = jnp.arange(span)
    causal = position[:, None] >= position[None, :]
    cumulative = jnp.cumsum(dt_rows * decay_rate[None, :], axis=0)
    b_wide = b_rows.astype(wide_type)
    c_wide = c_rows.astype(wide_type)
    x_wide = x_rows.astype(wide_type)
    products = jnp.dot(c_wide, b_wide.T, precision=highest)
    spread_log = cumulative.T[:, :, None] - cumulative.T[:, None, :]
    decays = jnp.exp(jnp.where(causal[None], spread_log, -jnp.inf))
    mixing = decays * products[None] * dt_rows.T[:, None, :]
    mixing = lax.optimization_barrier(mixing.astype(jnp.bfloat16)).astype(wide_type)
    outputs = jnp.einsum("hts,shp->thp", mixing, x_wide, precision=highest)
    state_low = lax.optimization_barrier(ssm_state.astype(jnp.bfloat16)).astype(wide_type)
    carried = jnp.einsum("hpn,tn->thp", state_low, c_wide, precision=highest)
    outputs = outputs + jnp.exp(cumulative)[:, :, None] * carried
    remaining = jnp.exp(cumulative[-1][None, :] - cumulative) * dt_rows
    weighted = x_wide * remaining[:, :, None]
    weighted = lax.optimization_barrier(weighted.astype(jnp.bfloat16)).astype(wide_type)
    ssm_state = jnp.exp(cumulative[-1])[:, None, None] * ssm_state + jnp.einsum("shp,sn->hpn", weighted, b_wide, precision=highest)
    return ssm_state, outputs


def mamba_part(ssm_x, ssm_z, ssm_bc, ssm_dt, a_log, d_skip, start_state, length, block_rows):
    row_count, full_width = ssm_x.shape
    head_count = ssm_dt.shape[1]
    head_dim = full_width // head_count
    state_dim = ssm_bc.shape[1] // 2
    block_rows = min(block_rows, row_count)
    blocks = row_count // block_rows
    live_rows = jnp.arange(row_count) < length
    dt_live = jnp.where(live_rows[:, None], ssm_dt, jnp.zeros_like(ssm_dt))
    decay_rate = -jnp.exp(a_log)
    x_wide = ssm_x.astype(ssm_dt.dtype).reshape(row_count, head_count, head_dim)
    x_parts = ssm_x.reshape(blocks, block_rows, head_count, head_dim)
    b_parts = ssm_bc[:, :state_dim].reshape(blocks, block_rows, state_dim)
    c_parts = ssm_bc[:, state_dim:].reshape(blocks, block_rows, state_dim)
    dt_parts = dt_live.reshape(blocks, block_rows, head_count)

    def fold_block(ssm_state, pieces):
        return advance(ssm_state, pieces[0], pieces[1], pieces[2], pieces[3], decay_rate)

    end_state, outputs = lax.scan(fold_block, start_state, (x_parts, b_parts, c_parts, dt_parts))
    outputs = outputs.reshape(row_count, head_count, head_dim) + d_skip[None, :, None] * x_wide
    gated = outputs.reshape(row_count, full_width) * jax.nn.silu(ssm_z.astype(ssm_dt.dtype))
    gated = jnp.where(live_rows[:, None], gated, jnp.zeros_like(gated)).astype(jnp.bfloat16)
    return gated, end_state


def reference(queries, suffix_kv, ssm_x, ssm_z, ssm_bc, ssm_dt, a_log, d_skip, prefix_kv, prefix_end_states, w_attn_out, w_ssm_out, suffix_len, prefix_of, prefix_owner):
    group_size = QH // KEY_VALUE_HEADS
    wide_type = ssm_dt.dtype

    def per_request(request):
        begin = (request * SUFFIX_TOKENS).astype(jnp.int32)
        length = suffix_len[request]
        slot_index = prefix_owner[prefix_of[request]].astype(jnp.int32)
        query_rows = lax.dynamic_slice_in_dim(queries, begin, SUFFIX_TOKENS, 0).astype(wide_type).reshape(SUFFIX_TOKENS, QH, HEAD_SIZE)
        cached = lax.dynamic_index_in_dim(prefix_kv, slot_index, 0, keepdims=False)
        fresh = lax.dynamic_slice_in_dim(suffix_kv, begin, SUFFIX_TOKENS, 0)
        all_kv = jnp.concatenate([cached, fresh], 0).astype(wide_type).reshape(PREFIX_LENGTH + SUFFIX_TOKENS, KEY_VALUE_HEADS, 2, HEAD_SIZE)
        key_rows = jnp.repeat(all_kv[:, :, 0], group_size, axis=1)
        value_rows = jnp.repeat(all_kv[:, :, 1], group_size, axis=1)
        scores = jnp.einsum("qhd,khd->hqk", query_rows, key_rows, precision=highest) * (HEAD_SIZE ** -0.5)
        query_pos = jnp.arange(SUFFIX_TOKENS)
        key_pos = jnp.arange(PREFIX_LENGTH + SUFFIX_TOKENS)
        allowed = (key_pos[None, :] < PREFIX_LENGTH) | (key_pos[None, :] - PREFIX_LENGTH <= query_pos[:, None])
        scores = jnp.where(allowed[None], scores, -jnp.inf)
        row_max = jnp.max(scores, axis=-1, keepdims=True)
        weights = jnp.exp(scores - row_max)
        row_sum = jnp.sum(weights, axis=-1)
        rounded = lax.optimization_barrier(weights.astype(jnp.bfloat16)).astype(wide_type)
        heads_out = jnp.einsum("hqk,khd->qhd", rounded, value_rows, precision=highest) / row_sum.T[:, :, None]
        live_rows = query_pos < length
        attention = heads_out.reshape(SUFFIX_TOKENS, QH * HEAD_SIZE)
        attention = jnp.where(live_rows[:, None], attention, jnp.zeros_like(attention)).astype(jnp.bfloat16)
        start_state = lax.dynamic_index_in_dim(prefix_end_states, slot_index, 0, keepdims=False).astype(wide_type)
        gated, end_state = mamba_part(
            lax.dynamic_slice_in_dim(ssm_x, begin, SUFFIX_TOKENS, 0),
            lax.dynamic_slice_in_dim(ssm_z, begin, SUFFIX_TOKENS, 0),
            lax.dynamic_slice_in_dim(ssm_bc, begin, SUFFIX_TOKENS, 0),
            lax.dynamic_slice_in_dim(ssm_dt, begin, SUFFIX_TOKENS, 0),
            a_log, d_skip, start_state, length, CH)
        return attention, gated, end_state

    attention, ssm_out, end_states = lax.map(per_request, jnp.arange(REQUEST_COUNT, dtype=jnp.int32))
    attention = attention.reshape(TOKENS, QH * HEAD_SIZE)
    ssm_out = ssm_out.reshape(TOKENS, MAMBA_HEADS * HEAD_SIZE)
    attn_share = QH * HEAD_SIZE // N_TP
    ssm_share = MAMBA_HEADS * HEAD_SIZE // N_TP
    mixed = jnp.zeros((TOKENS, D), wide_type)
    for member in range(N_TP):
        partial_sum = jnp.dot(attention[:, member * attn_share:(member + 1) * attn_share], w_attn_out[member * attn_share:(member + 1) * attn_share], preferred_element_type=jnp.float32)
        partial_sum = partial_sum + jnp.dot(ssm_out[:, member * ssm_share:(member + 1) * ssm_share], w_ssm_out[member * ssm_share:(member + 1) * ssm_share], preferred_element_type=jnp.float32)
        mixed = mixed + lax.optimization_barrier(partial_sum.astype(jnp.bfloat16)).astype(wide_type)
    return mixed.astype(jnp.bfloat16), end_states
```

```python
import jax
import jax.numpy as jnp
from jax import lax
from jax.experimental import pallas as pl
from jax.sharding import PartitionSpec as P

HEAD = 128
QH = 8
KVH = 2
REQ = 32
TP = 8
GROUP = 4
TAG_ROWS = 4
F32 = jnp.float32
BF16 = jnp.bfloat16


def exchange(value, axis, count, step):
    return lax.ppermute(value, axis, [(i, step(i)) for i in range(count)])


def split3(value):
    high = value.astype(BF16)
    rest = value - high.astype(F32)
    mid = rest.astype(BF16)
    low = (rest - mid.astype(F32)).astype(BF16)
    return high, mid, low


def spread_slots(prefix_kv, states, quarter, kv_head, prefix):
    rows = prefix_kv.shape[1] // GROUP
    piece = lax.dynamic_slice(
        prefix_kv[0], (quarter * rows, kv_head * 2 * HEAD), (rows, 2 * HEAD)
    )
    pieces = states[0].reshape(REQ, -1, 2 * HEAD)
    tag = jnp.broadcast_to(prefix.astype(BF16), (REQ, TAG_ROWS, 2 * HEAD))
    return jnp.concatenate([piece.reshape(REQ, -1, 2 * HEAD), pieces, tag], 1)


def pick_slots(chunks, prefix_owner):
    wanted = chunks[:, -1:, :].astype(F32)
    choice = lax.dynamic_index_in_dim(chunks, prefix_owner[0], 0)
    picked = jnp.broadcast_to(choice, chunks.shape)
    for prefix in range(1, prefix_owner.shape[0]):
        choice = lax.dynamic_index_in_dim(chunks, prefix_owner[prefix], 0)
        picked = jnp.where(wanted == prefix, choice, picked)
    return picked


def dot(left, right, contract):
    return lax.dot_general(left, right, (contract, ((), ())), preferred_element_type=F32)


def attention_kernel(q0, q1, q2, q3, cached, fresh, own_ref, log_ref, message_ref):
    keys = cached[:, :HEAD]
    values = cached[:, HEAD:]
    scale = HEAD ** (-0.5)
    for h, query in enumerate((q0, q1, q2, q3)):
        scores = dot(keys, query[...], ((1,), (1,))) * scale
        top = jnp.max(scores, 0, keepdims=True)
        if h == 0:
            own = dot(fresh[:, :HEAD], query[...], ((1,), (1,))) * scale
            key_at = lax.broadcasted_iota(jnp.int32, own.shape, 0)
            query_at = lax.broadcasted_iota(jnp.int32, own.shape, 1)
            own = jnp.where(key_at <= query_at, own, -jnp.inf)
            top = jnp.maximum(top, jnp.max(own, 0, keepdims=True))
        weights = jnp.exp(scores - top)
        total = jnp.sum(weights, 0, keepdims=True)
        out = dot(values, weights.astype(BF16), ((0,), (0,)))
        if h == 0:
            own = jnp.exp(own - top)
            total = total + jnp.sum(own, 0, keepdims=True)
            out = out + dot(fresh[:, HEAD:], own.astype(BF16), ((0,), (0,)))
        logs = top + jnp.log(total)
        normal = out / total
        if h == 0:
            own_ref[...] = normal
            log_ref[...] = logs
        else:
            high, mid, low = (part.astype(F32) for part in split3(logs))
            row = lax.broadcasted_iota(jnp.int32, (16, logs.shape[1]), 0)
            stats = jnp.where(row == 0, high, jnp.where(row == 1, mid, jnp.where(row == 2, low, 0.0)))
            message_ref[h - 1, :HEAD, :] = normal.astype(BF16)
            message_ref[h - 1, HEAD:, :] = stats.astype(BF16)


def body(
    queries,
    suffix_kv,
    ssm_x,
    ssm_z,
    ssm_bc,
    ssm_dt,
    a_log,
    d_skip,
    prefix_kv,
    prefix_end_states,
    w_attn_out,
    w_ssm_out,
    suffix_len,
    prefix_of,
    prefix_owner,
):
    tp = lax.axis_index("tp")
    rows = queries.shape[0]
    length = suffix_len[0]
    kv_head = tp // GROUP
    quarter = tp % GROUP

    with jax.named_scope("spread"):
        sent = spread_slots(prefix_kv, prefix_end_states, quarter, kv_head, prefix_of[0])
        chunks = lax.all_to_all(sent, "req", 0, 0)
    with jax.named_scope("queries_exchange"):
        heads = [queries] + [exchange(queries, "tp", TP, lambda i, k=k: i ^ k) for k in (1, 2, 3)]
    with jax.named_scope("fetch"):
        got = lax.all_to_all(pick_slots(chunks, prefix_owner), "req", 0, 0)
    key_rows = prefix_kv.shape[1] // GROUP // REQ
    cached = got[:, :key_rows].reshape(-1, 2 * HEAD)
    state = got[:, key_rows:-TAG_ROWS].reshape(prefix_end_states.shape[1:])

    with jax.named_scope("attention"):
        fresh = lax.dynamic_slice_in_dim(suffix_kv, kv_head * 2 * HEAD, 2 * HEAD, 1)
        normal, logs, messages = pl.pallas_call(
            attention_kernel,
            out_shape=(
                jax.ShapeDtypeStruct((HEAD, rows), F32),
                jax.ShapeDtypeStruct((1, rows), F32),
                jax.ShapeDtypeStruct((GROUP - 1, HEAD + 16, rows), BF16),
            ),
            name="attention_kernel",
        )(*heads, cached, fresh)
        arrived = [exchange(messages[k - 1], "tp", TP, lambda i, k=k: i ^ k) for k in (1, 2, 3)]

    with jax.named_scope("mamba"):
        position = jnp.arange(rows)
        live = position < length
        head_count = ssm_dt.shape[1]
        dt = jnp.where(live[:, None], ssm_dt, 0.0)
        rate = -jnp.exp(a_log)
        b_rows = ssm_bc[:, : 2 * HEAD]
        c_rows = ssm_bc[:, 2 * HEAD :]
        x = ssm_x.reshape(rows, head_count, HEAD)
        log_decay = jnp.cumsum(dt * rate[None, :], axis=0)
        back = position[:, None] >= position[None, :]
        products = jnp.dot(c_rows, b_rows.T, preferred_element_type=F32)
        diff = log_decay.T[:, :, None] - log_decay.T[:, None, :]
        decays = jnp.exp(jnp.where(back[None], diff, -jnp.inf))
        mixing = (decays * products[None] * dt.T[:, None, :]).astype(BF16)
        y = jnp.einsum("hts,shp->thp", mixing, x, preferred_element_type=F32)
        y = y + d_skip[None, :, None] * x.astype(F32)
        remaining = jnp.exp(log_decay[-1][None, :] - log_decay) * dt
        weighted = (x.astype(F32) * remaining[:, :, None]).astype(BF16)
        fresh_state = jnp.einsum("shp,sn->hpn", weighted, b_rows, preferred_element_type=F32)
        carried = jnp.einsum("hpn,tn->thp", state, c_rows, preferred_element_type=F32)
        y = y + jnp.exp(log_decay)[:, :, None] * carried
        end_state = jnp.exp(log_decay[-1])[:, None, None] * state.astype(F32) + fresh_state
        gated = y.reshape(rows, -1) * jax.nn.silu(ssm_z.astype(F32))
        gated = jnp.where(live[:, None], gated, 0.0).astype(BF16)
        gated_out = jnp.dot(gated, w_ssm_out, preferred_element_type=F32)
        arrived, gated_out = lax.optimization_barrier((arrived, gated_out))

    with jax.named_scope("combine"):
        other_logs = [jnp.sum(m[HEAD : HEAD + 3].astype(F32), 0) for m in arrived]
        all_logs = [logs[0]] + other_logs
        top = jnp.maximum(jnp.maximum(all_logs[0], all_logs[1]), jnp.maximum(all_logs[2], all_logs[3]))
        scale = [jnp.exp(v - top) for v in all_logs]
        total = scale[0] + scale[1] + scale[2] + scale[3]
        mixed_t = normal * scale[0]
        for k in range(3):
            mixed_t = mixed_t + arrived[k][:HEAD].astype(F32) * scale[k + 1]
        attention = (mixed_t / total).T
        attention = jnp.where(live[:, None], attention, 0.0).astype(BF16)

    with jax.named_scope("project"):
        partial = (
            jnp.dot(attention, w_attn_out, preferred_element_type=F32) + gated_out
        ).astype(BF16)
    with jax.named_scope("reduce"):
        mixed = reduce_rows(partial, tp)
    return mixed, end_state[None]


def reduce_rows(partial, tp):
    width = partial.shape[1]
    place = tp // 2
    core = tp % 2
    blocks = partial.reshape(4, 2, -1, width)
    keep = lax.dynamic_index_in_dim(blocks, core, 1, keepdims=False)
    give = lax.dynamic_index_in_dim(blocks, 1 - core, 1, keepdims=False)
    come = exchange(give, "tp", TP, lambda i: i ^ 1)
    chip = (keep.astype(F32) + come.astype(F32)).astype(BF16)
    half = chip.shape[1] // 2

    def part(offset, first):
        block = lax.dynamic_index_in_dim(chip, (place + offset) % 4, 0, keepdims=False)
        return block[:half] if first else block[half:]

    up = lambda value: exchange(value, "tp", TP, lambda i: (i + 2) % TP)
    down = lambda value: exchange(value, "tp", TP, lambda i: (i - 2) % TP)
    from_below = up(jnp.stack([part(2, True), part(1, False)]))
    from_above = down(jnp.stack([part(2, False), part(3, True)]))
    via_up = up((part(1, True).astype(F32) + from_below[0].astype(F32)).astype(BF16))
    via_down = down((part(3, False).astype(F32) + from_above[0].astype(F32)).astype(BF16))
    first = part(0, True).astype(F32) + via_up.astype(F32) + from_above[1].astype(F32)
    last = part(0, False).astype(F32) + via_down.astype(F32) + from_below[1].astype(F32)
    return jnp.concatenate([first, last], 0).astype(BF16)


def solution(mesh):
    in_specs = (
        P("req", "tp"),
        P("req", None),
        P("req", "tp"),
        P("req", "tp"),
        P("req", None),
        P("req", "tp"),
        P("tp"),
        P("tp"),
        P("req", None, None),
        P("req", "tp", None, None),
        P("tp", None),
        P("tp", None),
        P("req"),
        P("req"),
        P(),
    )
    out_specs = (P(("req", "tp"), None), P("req", "tp", None, None))
    return jax.shard_map(body, mesh=mesh, in_specs=in_specs, out_specs=out_specs, check_vma=False)
```
